768 devices in a mesh: lat: 24 (over z_lo, y), rad: 32 (over x, z_hi, core).
Axes of the slice: x: 4, y: 8, z: 12 (z_hi: 4, z_lo: 3; z = z_hi * 3 + z_lo), core: 2. Of those that a mesh axis runs over, the one named last changes fastest.
Arguments:
- displacement: float32 [3, 128, 1536, 384], P(None, 'rad', 'lat'), may hold values from -6 to 6
- forcing: float32 [3, 128, 1536, 384], P(None, 'rad', 'lat'), may hold values from -12 to 12
- layer_id: int32 [128], P('rad'), may hold values from 0 to 11
- stiffness: float32 [12], replicated, may hold values from 0.3 to 3
- coupling: float32 [12, 3, 3], replicated, may hold values from -0.5 to 0.5
- cycle_id: int32 [1536, 384], P('lat'), may hold values from 0 to 1535, as said below
- cycle_count: int32 [1536], replicated, may hold values from 192 to 576, as said below
- gravity: float32 [2, 2, 512], replicated, may hold values from -96 to 96
Outputs:
- smoothed: float32 [3, 128, 1536, 384], P(None, 'rad', 'lat')
- potential: float32 [2, 1536, 384], P(None, 'lat')
The draws below stay inside these ranges and needn't reach their ends.
Inputs may be any that keep to these rules, and one draw needn't show every extreme that they name: Every cycle holds at least one point, and cycle_id never falls along the lateral points taken row by row. cycle_count[j] is the number of points whose cycle_id is j.
All inputs are finite; a program needn't handle non-finite values.
Results may differ from the reference program's by a relative error of at most 0.0001.
Values sent between devices are 32-bit elements; how exact they have to be, the bound alone decides.
A program may use at most 64 MiB of HBM per device.

```python
import math
import jax
import jax.numpy as jnp
from jax import lax

QB = 384
SWEEPS = 2
NMAT = 12
NRING = 1536
L = 512
NR = 128
NA = 1536


def cycle_layout(key):
    base_key = jax.random.fold_in(key, 7)
    points = NA * QB
    base = points // NRING
    extra = points - base * NRING
    half = base // 2
    third = NRING // 3
    ranks = jnp.arange(NRING, dtype=jnp.int32)
    spread = jnp.where(ranks < third, half, jnp.where(ranks < 2 * third, 0, -half))
    spread = spread + (ranks < extra).astype(jnp.int32)
    order = jax.random.permutation(base_key, NRING).astype(jnp.int32)
    counts = (base + spread[order]).astype(jnp.int32)
    cycle_of = jnp.repeat(jnp.arange(NRING, dtype=jnp.int32), counts, total_repeat_length=points)
    return (cycle_of.reshape(NA, QB).astype(jnp.int32), counts)


def draw_cycle_id(key, part):
    return cycle_layout(key)[0]


def draw_cycle_count(key, part):
    return cycle_layout(key)[1]


def place_ends(values, key, low, top_value):
    place = [jax.random.randint(jax.random.fold_in(key, axis), (), 0, length) for axis, length in enumerate(values.shape)]
    main_axis = values.shape.index(max(values.shape))
    next_to = place[:main_axis] + [(place[main_axis] + 1) % values.shape[main_axis]] + place[main_axis + 1:]
    return values.at[tuple(place)].set(low).at[tuple(next_to)].set(top_value)


def levels(key, dims, pieces, least, high):
    factor_of, own = 1.0, jax.random.fold_in(key, 6)
    for axis_at, blocks in pieces:
        draws = jnp.exp(jax.random.uniform(jax.random.fold_in(own, axis_at), (blocks,), jnp.float32, least / len(pieces), high / len(pieces)))
        factor_of = factor_of * jnp.repeat(draws, dims[axis_at] // blocks).reshape([-1 if axis == axis_at else 1 for axis in range(len(dims))])
    return factor_of


def centred(rng, dims, deviation, reach, shards=(), kind=jnp.bfloat16):
    entries = jax.random.normal(rng, dims, jnp.float32) * deviation
    if len(shards) > 0:
        entries = levels(rng, dims, shards, -0.22, 0.18) * entries
    return jnp.clip(entries, min=-reach, max=reach).astype(kind)


def setup_inputs(seed: int = 0) -> dict:
    streams_of = jax.random.split(jax.random.key(seed), 9)
    return {
        "displacement": centred(streams_of[0], (3, NR, NA, QB), 1.0, 6.0, ((1, 32), (2, 24)), jnp.float32),
        "forcing": centred(streams_of[1], (3, NR, NA, QB), 2.0, 12.0, ((1, 32), (2, 24)), jnp.float32),
        "layer_id": place_ends(jax.random.randint(streams_of[2], (NR,), 0, NMAT), jax.random.fold_in(streams_of[2], 1), 0, NMAT - 1).astype(jnp.int32),
        "stiffness": jnp.clip(jnp.exp(jax.random.uniform(streams_of[3], (NMAT,), jnp.float32, math.log(0.3), math.log(3.0))), 0.3, 3.0),
        "coupling": jnp.clip(jax.random.uniform(streams_of[4], (NMAT, 3, 3), jnp.float32, -0.5, 0.5), -0.5, 0.5),
        "cycle_id": draw_cycle_id(jax.random.fold_in(streams_of[8], 71), 0),
        "cycle_count": draw_cycle_count(jax.random.fold_in(streams_of[8], 71), 0),
        "gravity": centred(streams_of[7], (2, 2, L), 16.0, 96.0, (), jnp.float32),
    }


OMEGA = 0.8
HIGHEST = lax.Precision.HIGHEST

def zonal_table(degrees, first_cycle, cycle_span, cycle_total):
    degree = jnp.arange(degrees, dtype=jnp.int32)[:, None]
    cycle_index = (first_cycle + jnp.arange(cycle_span, dtype=jnp.int32))[None, :]
    phases = degree * (2 * cycle_index + 1) % (4 * cycle_total)
    return jnp.cos(jnp.pi * phases.astype(jnp.float32) / (2.0 * cycle_total))

def apply_operator(padded, layer_mu, layer_coupling):
    center = padded[:, 1:-1, 1:-1, 1:-1]
    beside = padded[:, 2:, 1:-1, 1:-1] + padded[:, :-2, 1:-1, 1:-1]
    beside = beside + padded[:, 1:-1, 2:, 1:-1] + padded[:, 1:-1, :-2, 1:-1]
    beside = beside + padded[:, 1:-1, 1:-1, 2:] + padded[:, 1:-1, 1:-1, :-2]
    coupled = jnp.einsum('rcd,drab->crab', layer_coupling, center, precision=HIGHEST)
    return layer_mu[None, :, None, None] * (6.0 * center - beside) + coupled

def diagonal_of(layer_mu, layer_coupling):
    own = jnp.transpose(jnp.diagonal(layer_coupling, axis1=1, axis2=2))
    return 6.0 * layer_mu[None, :, None, None] + own[:, :, None, None]

def reference(displacement, forcing, layer_id, stiffness, coupling, cycle_id, cycle_count, gravity):
    layer_mu = stiffness[layer_id]
    layer_coupling = coupling[layer_id]
    diagonal = diagonal_of(layer_mu, layer_coupling)
    current = displacement
    for sweep_index in range(SWEEPS):
        padded = jnp.pad(current, ((0, 0), (1, 1), (1, 1), (1, 1)))
        current = current + OMEGA * (forcing - apply_operator(padded, layer_mu, layer_coupling)) / diagonal
    boundary = jnp.stack([current[0, -1], current[0, 0]])
    flat_ids = cycle_id.reshape(-1)
    cycle_sums = jax.vmap(lambda row_values: jax.ops.segment_sum(row_values, flat_ids, num_segments=NRING))(boundary.reshape(2, -1))
    cycle_means = cycle_sums / cycle_count.astype(jnp.float32)[None, :]
    basis = zonal_table(L, 0, NRING, NRING)
    scale = math.sqrt(2.0 / NRING)
    coefficients = scale * jnp.dot(cycle_means, basis.T, precision=HIGHEST)
    modes = gravity[:, 0] * coefficients[0][None, :] + gravity[:, 1] * coefficients[1][None, :]
    cycle_potential = scale * jnp.dot(modes, basis, precision=HIGHEST)
    potential = jnp.take(cycle_potential, cycle_id, axis=1)
    return (current, potential)
```

```python
import functools
import math

import jax
import jax.numpy as jnp
from jax import lax
from jax.experimental import pallas as pl
from jax.experimental.pallas import tpu as pltpu
from jax.sharding import PartitionSpec as P

OMEGA = 0.8
PAD = 8
CHUNKS = 4
SLOTS = 3
MESH = pl.DeviceIdType.MESH


def sides(padded, rows):
    width = padded.shape[1]
    up = pltpu.roll(padded, 1, 0)[PAD : PAD + rows]
    down = pltpu.roll(padded, rows + 2 * PAD - 1, 0)[PAD : PAD + rows]
    center = padded[PAD : PAD + rows]
    column = lax.broadcasted_iota(jnp.int32, center.shape, 1)
    left = jnp.where(column == 0, 0.0, pltpu.roll(center, 1, 1))
    right = jnp.where(column == width - 1, 0.0, pltpu.roll(center, width - 1, 1))
    return center, (up + down) + (left + right)


def relax(factors, layer, c, centers, beside, source):
    def factor(t):
        return factors[layer - 1, 4 * c + t : 4 * c + t + 1, :]

    own = (1.0 - OMEGA) * centers[c] + factor(0) * beside + factor(1) * source
    return own + factor(2) * centers[(c + 1) % 3] + factor(3) * centers[(c + 2) % 3]


def sweep_rows(field, factors, forces, layer, row, rows):
    centers, besides = [], []
    for c in range(3):
        padded = field[c, layer, pl.ds(row, rows + 2 * PAD), :]
        center, lateral = sides(padded, rows)
        inner = pl.ds(row + PAD, rows)
        besides.append(lateral + (field[c, layer - 1, inner, :] + field[c, layer + 1, inner, :]))
        centers.append(center)
    return [
        relax(factors, layer, c, centers, besides[c], forces[c, layer - 1, pl.ds(row, rows), :])
        for c in range(3)
    ]


def sine(z):
    z2 = z * z
    poly = 1.0
    for k in (6, 5, 4, 3, 2, 1):
        poly = 1.0 - poly * z2 * (1.0 / ((2 * k) * (2 * k + 1)))
    return z * poly


def kernel(
    sizes,
    disp, force, ids_in, count_in, gravity_in, layer_in, stiffness_in, coupling_in,
    smooth_out, pot_out,
    layer_id, stiffness, coupling, u0, u1, forces, ids, counts, gravity, factors, basis, plane, force_halo,
    weights, part_y, part_z, coef,
    load_sem, lat0_send, lat0_recv, fh_send, fh_recv, rad0_send, rad0_recv,
    rad1_send, rad1_recv, lat1_send, lat1_recv, y_send, y_recv, z_send, z_recv,
    coef_send, coef_recv,
):
    n_lat, n_rad, n_y = sizes
    n_z = n_lat // n_y
    depth, height = disp.shape[1], disp.shape[2]
    total = counts.shape[0]
    degrees = gravity.shape[2]
    rows = height // CHUNKS
    top = height + PAD
    lat = lax.axis_index("lat")
    rad = lax.axis_index("rad")
    y = lat % n_y
    z = lat // n_y
    has_low, has_high = lat > 0, lat < n_lat - 1
    has_below, has_above = rad > 0, rad < n_rad - 1
    at_end = jnp.logical_or(rad == 0, rad == n_rad - 1)
    is_top = rad // (n_rad - 1)
    edge = 1 + (depth - 1) * is_top
    within = 2 + (depth - 3) * is_top
    barrier = pltpu.get_barrier_semaphore()

    def greet(where):
        pl.semaphore_signal(barrier, inc=1, device_id=where, device_id_type=MESH)

    def remote(src, dst, send, recv, where):
        return pltpu.make_async_remote_copy(
            src_ref=src, dst_ref=dst, send_sem=send, recv_sem=recv,
            device_id=where, device_id_type=MESH,
        )

    loads = [
        pltpu.make_async_copy(disp, u0.at[:, 1 : depth + 1, PAD:top, :], load_sem.at[0]),
        pltpu.make_async_copy(force, forces, load_sem.at[1]),
        pltpu.make_async_copy(ids_in, ids, load_sem.at[2]),
        pltpu.make_async_copy(count_in, counts, load_sem.at[3]),
        pltpu.make_async_copy(gravity_in, gravity, load_sem.at[4]),
        pltpu.make_async_copy(layer_in, layer_id, load_sem.at[5]),
        pltpu.make_async_copy(stiffness_in, stiffness, load_sem.at[6]),
        pltpu.make_async_copy(coupling_in, coupling, load_sem.at[7]),
    ]

    @pl.when(has_low)
    def _():
        greet((lat - 1, rad))

    @pl.when(has_high)
    def _():
        greet((lat + 1, rad))

    @pl.when(has_below)
    def _():
        greet((lat, rad - 1))
        greet((lat, 0))

    @pl.when(has_above)
    def _():
        greet((lat, rad + 1))
        greet((lat, n_rad - 1))

    @pl.when(at_end)
    def _():
        @pl.loop(1, n_y)
        def _(i):
            greet((z * n_y + (y + i) % n_y, rad))

        @pl.loop(1, n_z)
        def _(i):
            greet((((z + i) % n_z) * n_y + y, rad))

    for load in loads:
        load.start()

    for field in (u0, u1):
        @pl.when(jnp.logical_not(has_low))
        def _():
            field[:, 1 : depth + 1, 0:PAD, :] = jnp.zeros((3, depth, PAD, disp.shape[3]), jnp.float32)

        @pl.when(jnp.logical_not(has_high))
        def _():
            field[:, 1 : depth + 1, top : top + PAD, :] = jnp.zeros((3, depth, PAD, disp.shape[3]), jnp.float32)

        @pl.when(jnp.logical_not(has_below))
        def _():
            field[:, 0] = jnp.zeros((3, top + PAD, disp.shape[3]), jnp.float32)

        @pl.when(jnp.logical_not(has_above))
        def _():
            field[:, depth + 1] = jnp.zeros((3, top + PAD, disp.shape[3]), jnp.float32)

    for load in loads:
        load.wait()

    wide = (1, disp.shape[3])
    materials = lax.broadcasted_iota(jnp.int32, (3, coupling.shape[2]), 1)
    for r in range(depth):
        mu = jnp.full(wide, stiffness[layer_id[r]], jnp.float32)
        for c in range(3):
            row = jnp.sum(
                jnp.where(materials == layer_id[r], coupling[c], 0.0), axis=1, keepdims=True
            )

            def pair(d):
                return jnp.broadcast_to(row[d : d + 1], wide)

            scale = OMEGA / (6.0 * mu + pair(c))
            factors[r, 4 * c : 4 * c + 1, :] = scale * mu
            factors[r, 4 * c + 1 : 4 * c + 2, :] = scale
            factors[r, 4 * c + 2 : 4 * c + 3, :] = -scale * pair((c + 1) % 3)
            factors[r, 4 * c + 3 : 4 * c + 4, :] = -scale * pair((c + 2) % 3)

    below = (rad + n_rad - 1) // n_rad
    above = (2 * n_rad - 2 - rad) // n_rad
    lateral = (lat + n_lat - 1) // n_lat + (2 * n_lat - 2 - lat) // n_lat
    peers = (n_y - 1) + (n_z - 1) + (n_rad - 1)
    pl.semaphore_wait(barrier, lateral + below + above + (1 - below * above) * peers)

    bottom_rows, top_rows = pl.ds(PAD, PAD), pl.ds(height, PAD)
    low_halo, high_halo = pl.ds(0, PAD), pl.ds(top, PAD)

    def lat_copies(field, layers, send, recv):
        layers = pl.ds(*layers)
        up = remote(
            field.at[:, layers, top_rows, :], field.at[:, layers, low_halo, :],
            send(0), recv(0), (lat + 1, rad),
        )
        down = remote(
            field.at[:, layers, bottom_rows, :], field.at[:, layers, high_halo, :],
            send(1), recv(1), (lat - 1, rad),
        )
        return up, down

    def force_copies():
        up = remote(
            forces.at[0, edge - 1, pl.ds(height - PAD, PAD), :], force_halo.at[0],
            fh_send.at[0], fh_recv.at[0], (lat + 1, rad),
        )
        down = remote(
            forces.at[0, edge - 1, pl.ds(0, PAD), :], force_halo.at[1],
            fh_send.at[1], fh_recv.at[1], (lat - 1, rad),
        )
        return up, down

    def start_lat(copies):
        up, down = copies

        @pl.when(has_high)
        def _():
            up.start()

        @pl.when(has_low)
        def _():
            down.start()

    def arrive_lat(copies):
        up, down = copies

        @pl.when(has_low)
        def _():
            up.wait_recv()

        @pl.when(has_high)
        def _():
            down.wait_recv()

    def leave_lat(copies):
        up, down = copies

        @pl.when(has_high)
        def _():
            up.wait_send()

        @pl.when(has_low)
        def _():
            down.wait_send()

    def chunk_of(i):
        return (CHUNKS - i) % CHUNKS

    def rad_up(field, send, recv, i):
        at = pl.ds(pl.multiple_of(PAD + chunk_of(i) * rows, 8), rows)
        return remote(
            field.at[:, depth, at, :], field.at[:, 0, at, :],
            send.at[0, i], recv.at[0, i], (lat, rad + 1),
        )

    def rad_down(field, send, recv, i):
        at = pl.ds(pl.multiple_of(PAD + chunk_of(i) * rows, 8), rows)
        return remote(
            field.at[:, 1, at, :], field.at[:, depth + 1, at, :],
            send.at[1, i], recv.at[1, i], (lat, rad - 1),
        )

    lat0 = lat_copies(u0, (1, depth), lambda d: lat0_send.at[d], lambda d: lat0_recv.at[d])
    start_lat(lat0)

    @pl.when(at_end)
    def _():
        start_lat(force_copies())

    for i in range(CHUNKS):
        @pl.when(has_above)
        def _():
            rad_up(u0, rad0_send, rad0_recv, i).start()

        @pl.when(has_below)
        def _():
            rad_down(u0, rad0_send, rad0_recv, i).start()

    first = ids[:, 0:1]
    degree = lax.broadcasted_iota(jnp.int32, (height, degrees), 1).astype(jnp.float32)
    period = 4.0 * total
    for k in range(SLOTS):
        odd = (2 * (first + k) + 1).astype(jnp.float32)
        phase = degree * odd
        phase = phase - period * jnp.floor(phase * (1.0 / period) + 0.5)
        basis[k] = sine((total - jnp.abs(phase)) * (math.pi / (2.0 * total)))

    @pl.when(at_end)
    def _():
        cycle = lax.broadcasted_iota(jnp.int32, (height, total), 1)
        for k in range(SLOTS):
            found = jnp.where(cycle == first + k, counts[...].reshape(1, total), 0)
            count = jnp.sum(found.astype(jnp.float32), axis=1, keepdims=True)
            weights[k] = jnp.where(count > 0.0, 1.0 / jnp.maximum(count, 1.0), 0.0)

    arrive_lat(lat0)

    @pl.loop(0, (depth - 2) * CHUNKS)
    def _(i):
        layer = 2 + i // CHUNKS
        row = pl.multiple_of((i % CHUNKS) * rows, 8)
        values = sweep_rows(u0, factors, forces, layer, row, rows)
        for c in range(3):
            u1[c, layer, pl.ds(row + PAD, rows), :] = values[c]

    lat1 = [
        lat_copies(
            u1, layers, lambda d, part=part: lat1_send.at[d, part],
            lambda d, part=part: lat1_recv.at[d, part],
        )
        for part, layers in enumerate(((2, depth - 2), (1, 1), (depth, 1)))
    ]
    start_lat(lat1[0])

    def y_copy(i):
        return remote(
            part_y.at[y], part_y.at[y], y_send.at[i], y_recv.at[y],
            (z * n_y + (y + i) % n_y, rad),
        )

    def y_arrival(i):
        other = (y + i) % n_y
        return remote(
            part_y.at[other], part_y.at[other], y_send.at[i], y_recv.at[other],
            (z * n_y + other, rad),
        )

    def z_copy(i):
        return remote(
            part_z.at[z], part_z.at[z], z_send.at[i], z_recv.at[z],
            (((z + i) % n_z) * n_y + y, rad),
        )

    def z_arrival(i):
        other = (z + i) % n_z
        return remote(
            part_z.at[other], part_z.at[other], z_send.at[i], z_recv.at[other],
            (other * n_y + y, rad),
        )

    def coef_copy(i):
        return remote(
            coef.at[is_top], coef.at[is_top], coef_send.at[i], coef_recv.at[is_top],
            (lat, (rad + i) % n_rad),
        )

    @pl.when(at_end)
    def _():
        arrive_lat(force_copies())

        @pl.loop(0, CHUNKS)
        def _(i):
            row = pl.multiple_of(i * rows, 8)
            values = sweep_rows(u0, factors, forces, edge, row, rows)
            for c in range(3):
                u1[c, edge, pl.ds(row + PAD, rows), :] = values[c]
            plane[pl.ds(row + PAD, rows), :] = values[0]

        for start, halo, inside in ((0, 0, has_low), (top, 1, has_high)):
            base = 0 if halo == 0 else top - PAD
            both = u0[0, edge, pl.ds(base, 2 * PAD), :]
            up = pltpu.roll(both, 1, 0)[start - base : start - base + PAD]
            down = pltpu.roll(both, 2 * PAD - 1, 0)[start - base : start - base + PAD]
            centers = [u0[c, edge, pl.ds(start, PAD), :] for c in range(3)]
            column = lax.broadcasted_iota(jnp.int32, centers[0].shape, 1)
            width = column.shape[1]
            left = jnp.where(column == 0, 0.0, pltpu.roll(centers[0], 1, 1))
            right = jnp.where(column == width - 1, 0.0, pltpu.roll(centers[0], width - 1, 1))
            beside = (up + down) + (left + right) + u0[0, within, pl.ds(start, PAD), :]
            value = relax(factors, edge, 0, centers, beside, force_halo[halo])
            plane[pl.ds(start, PAD), :] = jnp.where(inside, value, 0.0)

        center, lateral = sides(plane[...], height)
        own = pl.ds(PAD, height)
        centers = [center, u1[1, edge, own, :], u1[2, edge, own, :]]
        beside = lateral + u1[0, within, own, :]
        boundary = relax(factors, edge, 0, centers, beside, forces[0, edge - 1])
        partial = jnp.zeros((1, degrees), jnp.float32)
        for k in range(SLOTS):
            mine = jnp.where(ids[...] == first + k, boundary, 0.0)
            means = jnp.sum(mine, axis=1, keepdims=True) * weights[k]
            partial = partial + jnp.sum(means * basis[k], axis=0, keepdims=True)
        part_y[y] = partial

        @pl.loop(1, n_y)
        def _(i):
            y_copy(i).start()

    @pl.loop(0, CHUNKS)
    def _(i):
        row = pl.multiple_of(chunk_of(i) * rows, 8)

        @pl.when(has_above)
        def _():
            rad_down(u0, rad0_send, rad0_recv, i).wait_recv()

        values = sweep_rows(u0, factors, forces, depth, row, rows)
        for c in range(3):
            u1[c, depth, pl.ds(row + PAD, rows), :] = values[c]

        @pl.when(has_above)
        def _():
            rad_up(u1, rad1_send, rad1_recv, i).start()

        @pl.when(has_below)
        def _():
            rad_up(u0, rad0_send, rad0_recv, i).wait_recv()

        values = sweep_rows(u0, factors, forces, 1, row, rows)
        for c in range(3):
            u1[c, 1, pl.ds(row + PAD, rows), :] = values[c]

        @pl.when(has_below)
        def _():
            rad_down(u1, rad1_send, rad1_recv, i).start()

        @pl.when(i == 1)
        def _():
            start_lat(lat1[1])
            start_lat(lat1[2])

    @pl.when(at_end)
    def _():
        @pl.loop(1, n_y)
        def _(i):
            y_arrival(i).wait_recv()

        part_z[z] = jnp.sum(part_y[...], axis=0)

        @pl.loop(1, n_z)
        def _(i):
            z_copy(i).start()

    arrive_lat(lat1[0])

    @pl.loop(0, (depth - 2) * CHUNKS)
    def _(i):
        layer = 2 + i // CHUNKS
        row = pl.multiple_of((i % CHUNKS) * rows, 8)
        values = sweep_rows(u1, factors, forces, layer, row, rows)
        for c in range(3):
            smooth_out[c, layer - 1, pl.ds(row, rows), :] = values[c]

    scale = math.sqrt(2.0 / total)

    @pl.when(at_end)
    def _():
        @pl.loop(1, n_z)
        def _(i):
            z_arrival(i).wait_recv()

        coef[is_top] = scale * jnp.sum(part_z[...], axis=0)

        @pl.loop(1, n_rad)
        def _(i):
            coef_copy(i).start()

    arrive_lat(lat1[1])
    arrive_lat(lat1[2])

    @pl.loop(0, CHUNKS)
    def _(i):
        row = pl.multiple_of(chunk_of(i) * rows, 8)

        @pl.when(has_above)
        def _():
            rad_down(u1, rad1_send, rad1_recv, i).wait_recv()

        values = sweep_rows(u1, factors, forces, depth, row, rows)
        for c in range(3):
            smooth_out[c, depth - 1, pl.ds(row, rows), :] = values[c]

        @pl.when(has_below)
        def _():
            rad_up(u1, rad1_send, rad1_recv, i).wait_recv()

        values = sweep_rows(u1, factors, forces, 1, row, rows)
        for c in range(3):
            smooth_out[c, 0, pl.ds(row, rows), :] = values[c]

    def coef_arrival(side):
        return remote(
            coef.at[side], coef.at[side], coef_send.at[0], coef_recv.at[side],
            (lat, (rad + 1) % n_rad),
        )

    @pl.when(has_above)
    def _():
        coef_arrival(1).wait_recv()

    @pl.when(has_below)
    def _():
        coef_arrival(0).wait_recv()

    for k in range(2):
        modes = gravity[k, 0:1, :] * coef[1] + gravity[k, 1:2, :] * coef[0]
        values = [
            scale * jnp.sum(basis[s] * modes, axis=1, keepdims=True) for s in range(SLOTS)
        ]
        picked = jnp.where(ids[...] == first + 1, values[1], values[2])
        pot_out[k] = jnp.where(ids[...] == first, values[0], picked)

    leave_lat(lat0)
    for copies in lat1:
        leave_lat(copies)

    @pl.loop(0, CHUNKS)
    def _(i):
        @pl.when(has_above)
        def _():
            rad_up(u0, rad0_send, rad0_recv, i).wait_send()
            rad_up(u1, rad1_send, rad1_recv, i).wait_send()

        @pl.when(has_below)
        def _():
            rad_down(u0, rad0_send, rad0_recv, i).wait_send()
            rad_down(u1, rad1_send, rad1_recv, i).wait_send()

    @pl.when(at_end)
    def _():
        leave_lat(force_copies())

        @pl.loop(1, n_y)
        def _(i):
            y_copy(i).wait_send()

        @pl.loop(1, n_z)
        def _(i):
            z_copy(i).wait_send()

        @pl.loop(1, n_rad)
        def _(i):
            coef_copy(i).wait_send()


def solution(mesh):
    n_lat, n_rad = mesh.shape["lat"], mesh.shape["rad"]
    n_y = 8 if n_lat % 8 == 0 else max(1, n_lat // 2)
    n_z = n_lat // n_y

    def local(displacement, forcing, layer_id, stiffness, coupling, cycle_id, cycle_count, gravity):
        _, depth, height, width = displacement.shape
        total = cycle_count.shape[0]
        degrees = gravity.shape[2]
        vmem = pltpu.VMEM
        dma = pltpu.SemaphoreType.DMA
        f32 = jnp.float32
        field = vmem((3, depth + 2, height + 2 * PAD, width), f32)
        anywhere = pl.BlockSpec(memory_space=pl.ANY)
        inside = pl.BlockSpec(memory_space=pltpu.VMEM)
        return pl.pallas_call(
            functools.partial(kernel, (n_lat, n_rad, n_y)),
            out_shape=(
                jax.ShapeDtypeStruct(displacement.shape, f32),
                jax.ShapeDtypeStruct((2, height, width), f32),
            ),
            in_specs=[anywhere] * 8,
            out_specs=(inside, inside),
            scratch_shapes=[
                pltpu.SMEM(layer_id.shape, jnp.int32),
                pltpu.SMEM(stiffness.shape, f32),
                vmem((3, 3, stiffness.shape[0]), f32),
                field,
                field,
                vmem((3, depth, height, width), f32),
                vmem((height, width), jnp.int32),
                vmem((total,), jnp.int32),
                vmem((2, 2, degrees), f32),
                vmem((depth, 16, width), f32),
                vmem((SLOTS, height, degrees), f32),
                vmem((height + 2 * PAD, width), f32),
                vmem((2, PAD, width), f32),
                vmem((SLOTS, height, 1), f32),
                vmem((n_y, 1, degrees), f32),
                vmem((n_z, 1, degrees), f32),
                vmem((2, 1, degrees), f32),
                dma((8,)),
                dma((2,)), dma((2,)), dma((2,)), dma((2,)),
                dma((2, CHUNKS)), dma((2, CHUNKS)), dma((2, CHUNKS)), dma((2, CHUNKS)),
                dma((2, 3)), dma((2, 3)),
                dma((n_y,)), dma((n_y,)), dma((n_z,)), dma((n_z,)),
                dma((n_rad,)), dma((2,)),
            ],
            compiler_params=pltpu.CompilerParams(
                collective_id=0, has_side_effects=True, vmem_limit_bytes=40 << 20
            ),
        )(*(
            pltpu.with_memory_space_constraint(array, pltpu.HBM)
            for array in (
                displacement, forcing, cycle_id, cycle_count, gravity,
                layer_id, stiffness, jnp.transpose(coupling, (1, 2, 0)),
            )
        ))

    in_specs = (
        P(None, "rad", "lat", None),
        P(None, "rad", "lat", None),
        P("rad"),
        P(),
        P(),
        P("lat", None),
        P(),
        P(),
    )
    out_specs = (P(None, "rad", "lat", None), P(None, "lat", None))
    return jax.shard_map(local, mesh=mesh, in_specs=in_specs, out_specs=out_specs, check_vma=False)
```

```python
import functools
import math

import jax
import jax.numpy as jnp
from jax import lax
from jax.experimental import pallas as pl
from jax.experimental.pallas import tpu as pltpu
from jax.sharding import PartitionSpec as P

OMEGA = 0.8
PAD = 8
CHUNKS = 4
SLOTS = 3
MESH = pl.DeviceIdType.MESH


def sides(padded, rows):
    width = padded.shape[1]
    up = pltpu.roll(padded, 1, 0)[PAD : PAD + rows]
    down = pltpu.roll(padded, rows + 2 * PAD - 1, 0)[PAD : PAD + rows]
    center = padded[PAD : PAD + rows]
    column = lax.broadcasted_iota(jnp.int32, center.shape, 1)
    left = jnp.where(column == 0, 0.0, pltpu.roll(center, 1, 1))
    right = jnp.where(column == width - 1, 0.0, pltpu.roll(center, width - 1, 1))
    return center, (up + down) + (left + right)


def relax(factors, layer, c, centers, beside, source):
    def factor(t):
        return factors[layer - 1, 4 * c + t : 4 * c + t + 1, :]

    own = (1.0 - OMEGA) * centers[c] + factor(0) * beside + factor(1) * source
    return own + factor(2) * centers[(c + 1) % 3] + factor(3) * centers[(c + 2) % 3]


def sweep_rows(field, factors, forces, layer, row, rows, components=(0, 1, 2)):
    inner = pl.ds(row + PAD, rows)
    centers, besides = [], []
    for c in range(3):
        if c not in components:
            centers.append(field[c, layer, inner, :])
            besides.append(None)
            continue
        padded = field[c, layer, pl.ds(row, rows + 2 * PAD), :]
        center, lateral = sides(padded, rows)
        besides.append(lateral + (field[c, layer - 1, inner, :] + field[c, layer + 1, inner, :]))
        centers.append(center)
    return [
        relax(factors, layer, c, centers, besides[c], forces[c, layer - 1, pl.ds(row, rows), :])
        for c in components
    ]


def sine(z):
    z2 = z * z
    poly = 1.0
    for k in (6, 5, 4, 3, 2, 1):
        poly = 1.0 - poly * z2 * (1.0 / ((2 * k) * (2 * k + 1)))
    return z * poly


def kernel(
    sizes,
    disp, force, ids_in, count_in, gravity_in, layer_in, stiffness_in, coupling_in,
    smooth_out, pot_out,
    layer_id, stiffness, coupling, u0, u1, forces, ids, counts, gravity, factors, basis, plane, pack0, halo0,
    pack1, halo1, weights, part_y, part_z, coef,
    load_sem, lat0_send, lat0_recv, rad0_send, rad0_recv,
    rad1_send, rad1_recv, lat1_send, lat1_recv, y_send, y_recv, z_send, z_recv,
    coef_send, coef_recv,
):
    n_lat, n_rad, n_y = sizes
    n_z = n_lat // n_y
    depth, height = disp.shape[1], disp.shape[2]
    total = counts.shape[0]
    degrees = gravity.shape[2]
    rows = height // CHUNKS
    top = height + PAD
    lat = lax.axis_index("lat")
    rad = lax.axis_index("rad")
    y = lat % n_y
    z = lat // n_y
    has_low, has_high = lat > 0, lat < n_lat - 1
    has_below, has_above = rad > 0, rad < n_rad - 1
    at_end = jnp.logical_or(rad == 0, rad == n_rad - 1)
    is_top = rad // (n_rad - 1)
    edge = 1 + (depth - 1) * is_top
    within = 2 + (depth - 3) * is_top
    barrier = pltpu.get_barrier_semaphore()

    def greet(where):
        pl.semaphore_signal(barrier, inc=1, device_id=where, device_id_type=MESH)

    def remote(src, dst, send, recv, where):
        return pltpu.make_async_remote_copy(
            src_ref=src, dst_ref=dst, send_sem=send, recv_sem=recv,
            device_id=where, device_id_type=MESH,
        )

    loads = [
        pltpu.make_async_copy(disp, u0.at[:, 1 : depth + 1, PAD:top, :], load_sem.at[0]),
        pltpu.make_async_copy(force, forces, load_sem.at[1]),
        pltpu.make_async_copy(ids_in, ids, load_sem.at[2]),
        pltpu.make_async_copy(count_in, counts, load_sem.at[3]),
        pltpu.make_async_copy(gravity_in, gravity, load_sem.at[4]),
        pltpu.make_async_copy(layer_in, layer_id, load_sem.at[5]),
        pltpu.make_async_copy(stiffness_in, stiffness, load_sem.at[6]),
        pltpu.make_async_copy(coupling_in, coupling, load_sem.at[7]),
    ]

    @pl.when(has_low)
    def _():
        greet((lat - 1, rad))

    @pl.when(has_high)
    def _():
        greet((lat + 1, rad))

    @pl.when(has_below)
    def _():
        greet((lat, rad - 1))
        greet((lat, 0))

    @pl.when(has_above)
    def _():
        greet((lat, rad + 1))
        greet((lat, n_rad - 1))

    @pl.when(at_end)
    def _():
        @pl.loop(1, n_y)
        def _(i):
            greet((z * n_y + (y + i) % n_y, rad))

        @pl.loop(1, n_z)
        def _(i):
            greet((((z + i) % n_z) * n_y + y, rad))

    for load in loads:
        load.start()

    for field in (u0, u1):
        @pl.when(jnp.logical_not(has_low))
        def _():
            field[:, 1 : depth + 1, 0:PAD, :] = jnp.zeros((3, depth, PAD, disp.shape[3]), jnp.float32)

        @pl.when(jnp.logical_not(has_high))
        def _():
            field[:, 1 : depth + 1, top : top + PAD, :] = jnp.zeros((3, depth, PAD, disp.shape[3]), jnp.float32)

        @pl.when(jnp.logical_not(has_below))
        def _():
            field[:, 0] = jnp.zeros((3, top + PAD, disp.shape[3]), jnp.float32)

        @pl.when(jnp.logical_not(has_above))
        def _():
            field[:, depth + 1] = jnp.zeros((3, top + PAD, disp.shape[3]), jnp.float32)

    for load in loads:
        load.wait()

    wide = (1, disp.shape[3])
    materials = lax.broadcasted_iota(jnp.int32, (3, coupling.shape[2]), 1)
    for r in range(depth):
        mu = jnp.full(wide, stiffness[layer_id[r]], jnp.float32)
        for c in range(3):
            row = jnp.sum(
                jnp.where(materials == layer_id[r], coupling[c], 0.0), axis=1, keepdims=True
            )

            def pair(d):
                return jnp.broadcast_to(row[d : d + 1], wide)

            scale = OMEGA / (6.0 * mu + pair(c))
            factors[r, 4 * c : 4 * c + 1, :] = scale * mu
            factors[r, 4 * c + 1 : 4 * c + 2, :] = scale
            factors[r, 4 * c + 2 : 4 * c + 3, :] = -scale * pair((c + 1) % 3)
            factors[r, 4 * c + 3 : 4 * c + 4, :] = -scale * pair((c + 2) % 3)

    below = (rad + n_rad - 1) // n_rad
    above = (2 * n_rad - 2 - rad) // n_rad
    lateral = (lat + n_lat - 1) // n_lat + (2 * n_lat - 2 - lat) // n_lat
    peers = (n_y - 1) + (n_z - 1) + (n_rad - 1)

    def lat_up(pack, halo, send, recv):
        return remote(pack.at[0], halo.at[0], send.at[0], recv.at[0], (lat + 1, rad))

    def lat_down(pack, halo, send, recv):
        return remote(pack.at[1], halo.at[1], send.at[1], recv.at[1], (lat - 1, rad))

    lat0 = (pack0, halo0, lat0_send, lat0_recv)
    lat1 = [
        (pack1.at[part], halo1.at[part], lat1_send.at[part], lat1_recv.at[part])
        for part in range(2)
    ]
    all_layers = tuple(range(1, depth + 1))
    inner_layers, outer_layers = all_layers[1:-1], (1, depth)

    def planes(layers):
        return [(c, layer) for c in range(3) for layer in layers]

    def put_rows(field, pack, side, layers):
        row = PAD if side else top - 1
        for place, (c, layer) in enumerate(planes(layers)):
            pack[side, place : place + 1, :] = field[c, layer, row : row + 1, :]

    def take_rows(field, copies, layers):
        halo = copies[1]

        @pl.when(has_low)
        def _():
            lat_up(*copies).wait_recv()
            for place, (c, layer) in enumerate(planes(layers)):
                field[c, layer, PAD - 1 : PAD, :] = halo[0, place : place + 1, :]

        @pl.when(has_high)
        def _():
            lat_down(*copies).wait_recv()
            for place, (c, layer) in enumerate(planes(layers)):
                field[c, layer, top : top + 1, :] = halo[1, place : place + 1, :]

    def send_up(copies):
        @pl.when(has_high)
        def _():
            lat_up(*copies).start()

    def send_down(copies):
        @pl.when(has_low)
        def _():
            lat_down(*copies).start()

    def leave_lat(copies):
        @pl.when(has_high)
        def _():
            lat_up(*copies).wait_send()

        @pl.when(has_low)
        def _():
            lat_down(*copies).wait_send()

    def chunk_of(i):
        return (CHUNKS - i) % CHUNKS

    def rad_up(field, send, recv, i):
        at = pl.ds(pl.multiple_of(PAD + chunk_of(i) * rows, 8), rows)
        return remote(
            field.at[:, depth, at, :], field.at[:, 0, at, :],
            send.at[0, i], recv.at[0, i], (lat, rad + 1),
        )

    def rad_down(field, send, recv, i):
        at = pl.ds(pl.multiple_of(PAD + chunk_of(i) * rows, 8), rows)
        return remote(
            field.at[:, 1, at, :], field.at[:, depth + 1, at, :],
            send.at[1, i], recv.at[1, i], (lat, rad - 1),
        )

    spare = 3 * depth
    for side in range(2):
        put_rows(u0, pack0, side, all_layers)

    @pl.when(at_end)
    def _():
        for side, start in ((0, top - PAD), (1, PAD)):
            tile = pl.ds(start, PAD)
            centers = [u0[c, edge, tile, :] for c in range(3)]
            column = lax.broadcasted_iota(jnp.int32, centers[0].shape, 1)
            width = column.shape[1]
            left = jnp.where(column == 0, 0.0, pltpu.roll(centers[0], 1, 1))
            right = jnp.where(column == width - 1, 0.0, pltpu.roll(centers[0], width - 1, 1))
            along = pltpu.roll(centers[0], PAD - 1 if side else 1, 0)
            beside = along + (left + right) + u0[0, within, tile, :]
            value = relax(
                factors, edge, 0, centers, beside, forces[0, edge - 1, pl.ds(start - PAD, PAD), :]
            )
            pick = 0 if side else PAD - 1
            pack0[side, spare : spare + 1, :] = value[pick : pick + 1]

    pl.semaphore_wait(barrier, lateral + below + above + (1 - below * above) * peers)
    send_up(lat0)
    send_down(lat0)

    for i in range(CHUNKS):
        @pl.when(has_above)
        def _():
            rad_up(u0, rad0_send, rad0_recv, i).start()

        @pl.when(has_below)
        def _():
            rad_down(u0, rad0_send, rad0_recv, i).start()

    first = ids[:, 0:1]
    degree = lax.broadcasted_iota(jnp.int32, (height, degrees), 1).astype(jnp.float32)
    period = 4.0 * total
    for k in range(SLOTS):
        odd = (2 * (first + k) + 1).astype(jnp.float32)
        phase = degree * odd
        phase = phase - period * jnp.floor(phase * (1.0 / period) + 0.5)
        basis[k] = sine((total - jnp.abs(phase)) * (math.pi / (2.0 * total)))

    @pl.when(at_end)
    def _():
        cycle = lax.broadcasted_iota(jnp.int32, (height, total), 1)
        for k in range(SLOTS):
            found = jnp.where(cycle == first + k, counts[...].reshape(1, total), 0)
            count = jnp.sum(found.astype(jnp.float32), axis=1, keepdims=True)
            weights[k] = jnp.where(count > 0.0, 1.0 / jnp.maximum(count, 1.0), 0.0)

    take_rows(u0, lat0, all_layers)

    def y_copy(i):
        return remote(
            part_y.at[y], part_y.at[y], y_send.at[i], y_recv.at[y],
            (z * n_y + (y + i) % n_y, rad),
        )

    def y_arrival(i):
        other = (y + i) % n_y
        return remote(
            part_y.at[other], part_y.at[other], y_send.at[i], y_recv.at[other],
            (z * n_y + other, rad),
        )

    def z_copy(i):
        return remote(
            part_z.at[z], part_z.at[z], z_send.at[i], z_recv.at[z],
            (((z + i) % n_z) * n_y + y, rad),
        )

    def z_arrival(i):
        other = (z + i) % n_z
        return remote(
            part_z.at[other], part_z.at[other], z_send.at[i], z_recv.at[other],
            (other * n_y + y, rad),
        )

    def coef_copy(i):
        return remote(
            coef.at[is_top], coef.at[is_top], coef_send.at[i], coef_recv.at[is_top],
            (lat, (rad + i) % n_rad),
        )

    @pl.when(at_end)
    def _():
        @pl.loop(0, CHUNKS)
        def _(i):
            row = pl.multiple_of(i * rows, 8)
            values = sweep_rows(u0, factors, forces, edge, row, rows)
            for c in range(3):
                u1[c, edge, pl.ds(row + PAD, rows), :] = values[c]
            plane[pl.ds(row + PAD, rows), :] = values[0]
            values = sweep_rows(u0, factors, forces, within, row, rows, (0,))
            u1[0, within, pl.ds(row + PAD, rows), :] = values[0]

        for side, inside, row, own in ((0, has_low, PAD - 1, PAD), (1, has_high, top, top - 1)):
            value = halo0[side, spare : spare + 1, :]
            value = value + factors[edge - 1, 0:1, :] * u0[0, edge, own : own + 1, :]
            plane[row : row + 1, :] = jnp.where(inside, value, 0.0)

        center, lateral = sides(plane[...], height)
        own = pl.ds(PAD, height)
        centers = [center, u1[1, edge, own, :], u1[2, edge, own, :]]
        beside = lateral + u1[0, within, own, :]
        boundary = relax(factors, edge, 0, centers, beside, forces[0, edge - 1])
        partial = jnp.zeros((1, degrees), jnp.float32)
        for k in range(SLOTS):
            mine = jnp.where(ids[...] == first + k, boundary, 0.0)
            means = jnp.sum(mine, axis=1, keepdims=True) * weights[k]
            partial = partial + jnp.sum(means * basis[k], axis=0, keepdims=True)
        part_y[y] = partial

        @pl.loop(1, n_y)
        def _(i):
            y_copy(i).start()

    @pl.loop(0, (depth - 2) * CHUNKS)
    def _(i):
        layer = 2 + i // CHUNKS
        row = pl.multiple_of((i % CHUNKS) * rows, 8)
        values = sweep_rows(u0, factors, forces, layer, row, rows)
        for c in range(3):
            u1[c, layer, pl.ds(row + PAD, rows), :] = values[c]

    for side in range(2):
        put_rows(u1, pack1.at[0], side, inner_layers)
    send_up(lat1[0])
    send_down(lat1[0])

    @pl.loop(0, CHUNKS)
    def _(i):
        row = pl.multiple_of(chunk_of(i) * rows, 8)

        @pl.when(has_above)
        def _():
            rad_down(u0, rad0_send, rad0_recv, i).wait_recv()

        values = sweep_rows(u0, factors, forces, depth, row, rows)
        for c in range(3):
            u1[c, depth, pl.ds(row + PAD, rows), :] = values[c]

        @pl.when(has_above)
        def _():
            rad_up(u1, rad1_send, rad1_recv, i).start()

        @pl.when(has_below)
        def _():
            rad_up(u0, rad0_send, rad0_recv, i).wait_recv()

        values = sweep_rows(u0, factors, forces, 1, row, rows)
        for c in range(3):
            u1[c, 1, pl.ds(row + PAD, rows), :] = values[c]

        @pl.when(has_below)
        def _():
            rad_down(u1, rad1_send, rad1_recv, i).start()

        @pl.when(i == 0)
        def _():
            put_rows(u1, pack1.at[1], 1, outer_layers)
            send_down(lat1[1])

        @pl.when(i == 1)
        def _():
            put_rows(u1, pack1.at[1], 0, outer_layers)
            send_up(lat1[1])

    @pl.when(at_end)
    def _():
        @pl.loop(1, n_y)
        def _(i):
            y_arrival(i).wait_recv()

        part_z[z] = jnp.sum(part_y[...], axis=0)

        @pl.loop(1, n_z)
        def _(i):
            z_copy(i).start()

    take_rows(u1, lat1[0], inner_layers)

    @pl.loop(0, (depth - 2) * CHUNKS)
    def _(i):
        layer = 2 + i // CHUNKS
        row = pl.multiple_of((i % CHUNKS) * rows, 8)
        values = sweep_rows(u1, factors, forces, layer, row, rows)
        for c in range(3):
            smooth_out[c, layer - 1, pl.ds(row, rows), :] = values[c]

    scale = math.sqrt(2.0 / total)

    @pl.when(at_end)
    def _():
        @pl.loop(1, n_z)
        def _(i):
            z_arrival(i).wait_recv()

        coef[is_top] = scale * jnp.sum(part_z[...], axis=0)

        @pl.loop(1, n_rad)
        def _(i):
            coef_copy(i).start()

    take_rows(u1, lat1[1], outer_layers)

    @pl.loop(0, CHUNKS)
    def _(i):
        row = pl.multiple_of(chunk_of(i) * rows, 8)

        @pl.when(has_above)
        def _():
            rad_down(u1, rad1_send, rad1_recv, i).wait_recv()

        values = sweep_rows(u1, factors, forces, depth, row, rows)
        for c in range(3):
            smooth_out[c, depth - 1, pl.ds(row, rows), :] = values[c]

        @pl.when(has_below)
        def _():
            rad_up(u1, rad1_send, rad1_recv, i).wait_recv()

        values = sweep_rows(u1, factors, forces, 1, row, rows)
        for c in range(3):
            smooth_out[c, 0, pl.ds(row, rows), :] = values[c]

    def coef_arrival(side):
        return remote(
            coef.at[side], coef.at[side], coef_send.at[0], coef_recv.at[side],
            (lat, (rad + 1) % n_rad),
        )

    @pl.when(has_above)
    def _():
        coef_arrival(1).wait_recv()

    @pl.when(has_below)
    def _():
        coef_arrival(0).wait_recv()

    for k in range(2):
        modes = gravity[k, 0:1, :] * coef[1] + gravity[k, 1:2, :] * coef[0]
        values = [
            scale * jnp.sum(basis[s] * modes, axis=1, keepdims=True) for s in range(SLOTS)
        ]
        picked = jnp.where(ids[...] == first + 1, values[1], values[2])
        pot_out[k] = jnp.where(ids[...] == first, values[0], picked)

    leave_lat(lat0)
    for copies in lat1:
        leave_lat(copies)

    @pl.loop(0, CHUNKS)
    def _(i):
        @pl.when(has_above)
        def _():
            rad_up(u0, rad0_send, rad0_recv, i).wait_send()
            rad_up(u1, rad1_send, rad1_recv, i).wait_send()

        @pl.when(has_below)
        def _():
            rad_down(u0, rad0_send, rad0_recv, i).wait_send()
            rad_down(u1, rad1_send, rad1_recv, i).wait_send()

    @pl.when(at_end)
    def _():
        @pl.loop(1, n_y)
        def _(i):
            y_copy(i).wait_send()

        @pl.loop(1, n_z)
        def _(i):
            z_copy(i).wait_send()

        @pl.loop(1, n_rad)
        def _(i):
            coef_copy(i).wait_send()


def solution(mesh):
    n_lat, n_rad = mesh.shape["lat"], mesh.shape["rad"]
    n_y = 8 if n_lat % 8 == 0 else max(1, n_lat // 2)
    n_z = n_lat // n_y

    def local(displacement, forcing, layer_id, stiffness, coupling, cycle_id, cycle_count, gravity):
        _, depth, height, width = displacement.shape
        total = cycle_count.shape[0]
        degrees = gravity.shape[2]
        vmem = pltpu.VMEM
        dma = pltpu.SemaphoreType.DMA
        f32 = jnp.float32
        field = vmem((3, depth + 2, height + 2 * PAD, width), f32)
        anywhere = pl.BlockSpec(memory_space=pl.ANY)
        inside = pl.BlockSpec(memory_space=pltpu.VMEM)
        return pl.pallas_call(
            functools.partial(kernel, (n_lat, n_rad, n_y)),
            out_shape=(
                jax.ShapeDtypeStruct(displacement.shape, f32),
                jax.ShapeDtypeStruct((2, height, width), f32),
            ),
            in_specs=[anywhere] * 8,
            out_specs=(inside, inside),
            scratch_shapes=[
                pltpu.SMEM(layer_id.shape, jnp.int32),
                pltpu.SMEM(stiffness.shape, f32),
                vmem((3, 3, stiffness.shape[0]), f32),
                field,
                field,
                vmem((3, depth, height, width), f32),
                vmem((height, width), jnp.int32),
                vmem((total,), jnp.int32),
                vmem((2, 2, degrees), f32),
                vmem((depth, 16, width), f32),
                vmem((SLOTS, height, degrees), f32),
                vmem((height + 2 * PAD, width), f32),
                vmem((2, 16, width), f32),
                vmem((2, 16, width), f32),
                vmem((2, 2, 8, width), f32),
                vmem((2, 2, 8, width), f32),
                vmem((SLOTS, height, 1), f32),
                vmem((n_y, 1, degrees), f32),
                vmem((n_z, 1, degrees), f32),
                vmem((2, 1, degrees), f32),
                dma((8,)),
                dma((2,)), dma((2,)),
                dma((2, CHUNKS)), dma((2, CHUNKS)), dma((2, CHUNKS)), dma((2, CHUNKS)),
                dma((2, 2)), dma((2, 2)),
                dma((n_y,)), dma((n_y,)), dma((n_z,)), dma((n_z,)),
                dma((n_rad,)), dma((2,)),
            ],
            compiler_params=pltpu.CompilerParams(
                collective_id=0, has_side_effects=True, vmem_limit_bytes=40 << 20
            ),
        )(*(
            pltpu.with_memory_space_constraint(array, pltpu.HBM)
            for array in (
                displacement, forcing, cycle_id, cycle_count, gravity,
                layer_id, stiffness, jnp.transpose(coupling, (1, 2, 0)),
            )
        ))

    in_specs = (
        P(None, "rad", "lat", None),
        P(None, "rad", "lat", None),
        P("rad"),
        P(),
        P(),
        P("lat", None),
        P(),
        P(),
    )
    out_specs = (P(None, "rad", "lat", None), P(None, "lat", None))
    return jax.shard_map(local, mesh=mesh, in_specs=in_specs, out_specs=out_specs, check_vma=False)
```

```python
import functools
import math

import jax
import jax.numpy as jnp
from jax import lax
from jax.experimental import pallas as pl
from jax.experimental.pallas import tpu as pltpu
from jax.sharding import PartitionSpec as P

OMEGA = 0.8
PAD = 8
CHUNKS = 4
SLOTS = 3
MESH = pl.DeviceIdType.MESH


def sides(padded, rows):
    width = padded.shape[1]
    up = pltpu.roll(padded, 1, 0)[PAD : PAD + rows]
    down = pltpu.roll(padded, rows + 2 * PAD - 1, 0)[PAD : PAD + rows]
    center = padded[PAD : PAD + rows]
    column = lax.broadcasted_iota(jnp.int32, center.shape, 1)
    left = jnp.where(column == 0, 0.0, pltpu.roll(center, 1, 1))
    right = jnp.where(column == width - 1, 0.0, pltpu.roll(center, width - 1, 1))
    return center, (up + down) + (left + right)


def relax(factors, layer, c, centers, beside, source):
    def factor(t):
        return factors[layer - 1, 4 * c + t : 4 * c + t + 1, :]

    own = (1.0 - OMEGA) * centers[c] + factor(0) * beside + factor(1) * source
    return own + factor(2) * centers[(c + 1) % 3] + factor(3) * centers[(c + 2) % 3]


def sweep_rows(field, factors, forces, layer, row, rows, components=(0, 1, 2)):
    inner = pl.ds(row + PAD, rows)
    centers, besides = [], []
    for c in range(3):
        if c not in components:
            centers.append(field[c, layer, inner, :])
            besides.append(None)
            continue
        padded = field[c, layer, pl.ds(row, rows + 2 * PAD), :]
        center, lateral = sides(padded, rows)
        besides.append(lateral + (field[c, layer - 1, inner, :] + field[c, layer + 1, inner, :]))
        centers.append(center)
    return [
        relax(factors, layer, c, centers, besides[c], forces[c, layer - 1, pl.ds(row, rows), :])
        for c in components
    ]


def sine(z):
    z2 = z * z
    poly = 1.0
    for k in (6, 5, 4, 3, 2, 1):
        poly = 1.0 - poly * z2 * (1.0 / ((2 * k) * (2 * k + 1)))
    return z * poly


def kernel(
    sizes,
    disp, force, ids_in, count_in, gravity_in, layer_in, stiffness_in, coupling_in,
    smooth_out, pot_out,
    layer_id, stiffness, coupling, u0, u1, forces, ids, counts, gravity, factors, basis, plane, pack0, halo0,
    pack1, halo1, weights, part, coef,
    load_sem, lat0_send, lat0_recv, rad0_send, rad0_recv,
    rad1_send, rad1_recv, lat1_send, lat1_recv, part_send, part_recv,
    coef_send, coef_recv,
):
    n_lat, n_rad = sizes
    depth, height = disp.shape[1], disp.shape[2]
    total = counts.shape[0]
    degrees = gravity.shape[2]
    rows = height // CHUNKS
    top = height + PAD
    lat = lax.axis_index("lat")
    rad = lax.axis_index("rad")
    has_low, has_high = lat > 0, lat < n_lat - 1
    has_below, has_above = rad > 0, rad < n_rad - 1
    at_end = jnp.logical_or(rad == 0, rad == n_rad - 1)
    is_top = rad // (n_rad - 1)
    edge = 1 + (depth - 1) * is_top
    within = 2 + (depth - 3) * is_top
    barrier = pltpu.get_barrier_semaphore()

    def greet(where):
        pl.semaphore_signal(barrier, inc=1, device_id=where, device_id_type=MESH)

    def remote(src, dst, send, recv, where):
        return pltpu.make_async_remote_copy(
            src_ref=src, dst_ref=dst, send_sem=send, recv_sem=recv,
            device_id=where, device_id_type=MESH,
        )

    loads = [
        pltpu.make_async_copy(disp, u0.at[:, 1 : depth + 1, PAD:top, :], load_sem.at[0]),
        pltpu.make_async_copy(force, forces, load_sem.at[1]),
        pltpu.make_async_copy(ids_in, ids, load_sem.at[2]),
        pltpu.make_async_copy(count_in, counts, load_sem.at[3]),
        pltpu.make_async_copy(gravity_in, gravity, load_sem.at[4]),
        pltpu.make_async_copy(layer_in, layer_id, load_sem.at[5]),
        pltpu.make_async_copy(stiffness_in, stiffness, load_sem.at[6]),
        pltpu.make_async_copy(coupling_in, coupling, load_sem.at[7]),
    ]

    @pl.when(has_low)
    def _():
        greet((lat - 1, rad))

    @pl.when(has_high)
    def _():
        greet((lat + 1, rad))

    @pl.when(has_below)
    def _():
        greet((lat, rad - 1))
        greet((lat, 0))

    @pl.when(has_above)
    def _():
        greet((lat, rad + 1))
        greet((lat, n_rad - 1))

    @pl.when(at_end)
    def _():
        @pl.loop(1, n_lat)
        def _(i):
            greet(((lat + i) % n_lat, rad))

    for load in loads[5:] + loads[:5]:
        load.start()

    for field in (u0, u1):
        @pl.when(jnp.logical_not(has_low))
        def _():
            field[:, 1 : depth + 1, 0:PAD, :] = jnp.zeros((3, depth, PAD, disp.shape[3]), jnp.float32)

        @pl.when(jnp.logical_not(has_high))
        def _():
            field[:, 1 : depth + 1, top : top + PAD, :] = jnp.zeros((3, depth, PAD, disp.shape[3]), jnp.float32)

        @pl.when(jnp.logical_not(has_below))
        def _():
            field[:, 0] = jnp.zeros((3, top + PAD, disp.shape[3]), jnp.float32)

        @pl.when(jnp.logical_not(has_above))
        def _():
            field[:, depth + 1] = jnp.zeros((3, top + PAD, disp.shape[3]), jnp.float32)

    for load in loads[5:]:
        load.wait()

    wide = (1, disp.shape[3])
    materials = lax.broadcasted_iota(jnp.int32, (3, coupling.shape[2]), 1)
    for r in range(depth):
        mu = jnp.full(wide, stiffness[layer_id[r]], jnp.float32)
        for c in range(3):
            row = jnp.sum(
                jnp.where(materials == layer_id[r], coupling[c], 0.0), axis=1, keepdims=True
            )

            def pair(d):
                return jnp.broadcast_to(row[d : d + 1], wide)

            scale = OMEGA / (6.0 * mu + pair(c))
            factors[r, 4 * c : 4 * c + 1, :] = scale * mu
            factors[r, 4 * c + 1 : 4 * c + 2, :] = scale
            factors[r, 4 * c + 2 : 4 * c + 3, :] = -scale * pair((c + 1) % 3)
            factors[r, 4 * c + 3 : 4 * c + 4, :] = -scale * pair((c + 2) % 3)

    below = (rad + n_rad - 1) // n_rad
    above = (2 * n_rad - 2 - rad) // n_rad
    lateral = (lat + n_lat - 1) // n_lat + (2 * n_lat - 2 - lat) // n_lat
    peers = (n_lat - 1) + (n_rad - 1)

    def lat_up(pack, halo, send, recv):
        return remote(pack.at[0], halo.at[0], send.at[0], recv.at[0], (lat + 1, rad))

    def lat_down(pack, halo, send, recv):
        return remote(pack.at[1], halo.at[1], send.at[1], recv.at[1], (lat - 1, rad))

    lat0 = (pack0, halo0, lat0_send, lat0_recv)
    lat1 = [
        (pack1.at[part], halo1.at[part], lat1_send.at[part], lat1_recv.at[part])
        for part in range(2)
    ]
    all_layers = tuple(range(1, depth + 1))
    inner_layers, outer_layers = all_layers[1:-1], (1, depth)

    def planes(layers):
        return [(c, layer) for c in range(3) for layer in layers]

    def put_rows(field, pack, side, layers):
        row = PAD if side else top - 1
        for place, (c, layer) in enumerate(planes(layers)):
            pack[side, place : place + 1, :] = field[c, layer, row : row + 1, :]

    def take_rows(field, copies, layers):
        halo = copies[1]

        @pl.when(has_low)
        def _():
            lat_up(*copies).wait_recv()
            for place, (c, layer) in enumerate(planes(layers)):
                field[c, layer, PAD - 1 : PAD, :] = halo[0, place : place + 1, :]

        @pl.when(has_high)
        def _():
            lat_down(*copies).wait_recv()
            for place, (c, layer) in enumerate(planes(layers)):
                field[c, layer, top : top + 1, :] = halo[1, place : place + 1, :]

    def send_up(copies):
        @pl.when(has_high)
        def _():
            lat_up(*copies).start()

    def send_down(copies):
        @pl.when(has_low)
        def _():
            lat_down(*copies).start()

    def leave_lat(copies):
        @pl.when(has_high)
        def _():
            lat_up(*copies).wait_send()

        @pl.when(has_low)
        def _():
            lat_down(*copies).wait_send()

    def chunk_of(i):
        return i + 1 - 2 * (i % 2)

    def rad_up(i):
        at = pl.ds(pl.multiple_of(PAD + chunk_of(i) * rows, 8), rows)
        return remote(
            u1.at[:, depth, at, :], u1.at[:, 0, at, :],
            rad1_send.at[0, i], rad1_recv.at[0, i], (lat, rad + 1),
        )

    def rad_up_first(i):
        start = chunk_of(i) * rows
        return remote(
            disp.at[:, depth - 1, pl.ds(start, rows), :],
            u0.at[:, 0, pl.ds(pl.multiple_of(PAD + start, 8), rows), :],
            rad0_send.at[0, i], rad0_recv.at[0, i], (lat, rad + 1),
        )

    def rad_down_first(i):
        start = chunk_of(i) * rows
        return remote(
            disp.at[:, 0, pl.ds(start, rows), :],
            u0.at[:, depth + 1, pl.ds(pl.multiple_of(PAD + start, 8), rows), :],
            rad0_send.at[1, i], rad0_recv.at[1, i], (lat, rad - 1),
        )

    def rad_down(i):
        at = pl.ds(pl.multiple_of(PAD + chunk_of(i) * rows, 8), rows)
        return remote(
            u1.at[:, 1, at, :], u1.at[:, depth + 1, at, :],
            rad1_send.at[1, i], rad1_recv.at[1, i], (lat, rad - 1),
        )

    pl.semaphore_wait(barrier, lateral + below + above + (1 - below * above) * peers)
    def send_first(chunks):
        for i in chunks:
            @pl.when(has_above)
            def _():
                rad_up_first(i).start()

            @pl.when(has_below)
            def _():
                rad_down_first(i).start()

    send_first(range(1))
    for load in loads[:5]:
        load.wait()

    spare = 3 * depth
    for side in range(2):
        put_rows(u0, pack0, side, all_layers)

    @pl.when(at_end)
    def _():
        for side, start in ((0, top - PAD), (1, PAD)):
            tile = pl.ds(start, PAD)
            centers = [u0[c, edge, tile, :] for c in range(3)]
            column = lax.broadcasted_iota(jnp.int32, centers[0].shape, 1)
            width = column.shape[1]
            left = jnp.where(column == 0, 0.0, pltpu.roll(centers[0], 1, 1))
            right = jnp.where(column == width - 1, 0.0, pltpu.roll(centers[0], width - 1, 1))
            along = pltpu.roll(centers[0], PAD - 1 if side else 1, 0)
            beside = along + (left + right) + u0[0, within, tile, :]
            value = relax(
                factors, edge, 0, centers, beside, forces[0, edge - 1, pl.ds(start - PAD, PAD), :]
            )
            pick = 0 if side else PAD - 1
            pack0[side, spare : spare + 1, :] = value[pick : pick + 1]

    send_up(lat0)
    send_down(lat0)
    send_first(range(1, CHUNKS))

    first = ids[:, 0:1]
    degree = lax.broadcasted_iota(jnp.int32, (height, degrees), 1).astype(jnp.float32)
    period = 4.0 * total
    for k in range(SLOTS):
        odd = (2 * (first + k) + 1).astype(jnp.float32)
        phase = degree * odd
        phase = phase - period * jnp.floor(phase * (1.0 / period) + 0.5)
        basis[k] = sine((total - jnp.abs(phase)) * (math.pi / (2.0 * total)))

    @pl.when(at_end)
    def _():
        cycle = lax.broadcasted_iota(jnp.int32, (height, total), 1)
        for k in range(SLOTS):
            found = jnp.where(cycle == first + k, counts[...].reshape(1, total), 0)
            count = jnp.sum(found.astype(jnp.float32), axis=1, keepdims=True)
            weights[k] = jnp.where(count > 0.0, 1.0 / jnp.maximum(count, 1.0), 0.0)

    def part_copy(i):
        return remote(
            part.at[lat], part.at[lat], part_send.at[i], part_recv.at[lat],
            ((lat + i) % n_lat, rad),
        )

    def part_arrival(i):
        other = (lat + i) % n_lat
        return remote(
            part.at[other], part.at[other], part_send.at[i], part_recv.at[other], (other, rad)
        )

    def coef_copy(i):
        return remote(
            coef.at[is_top], coef.at[is_top], coef_send.at[i], coef_recv.at[is_top],
            (lat, (rad + i) % n_rad),
        )

    @pl.when(at_end)
    def _():
        take_rows(u0, lat0, all_layers)

        @pl.loop(0, CHUNKS)
        def _(i):
            row = pl.multiple_of(i * rows, 8)
            values = sweep_rows(u0, factors, forces, edge, row, rows)
            for c in range(3):
                u1[c, edge, pl.ds(row + PAD, rows), :] = values[c]
            plane[pl.ds(row + PAD, rows), :] = values[0]
            values = sweep_rows(u0, factors, forces, within, row, rows, (0,))
            u1[0, within, pl.ds(row + PAD, rows), :] = values[0]

        for side, inside, row, own in ((0, has_low, PAD - 1, PAD), (1, has_high, top, top - 1)):
            value = halo0[side, spare : spare + 1, :]
            value = value + factors[edge - 1, 0:1, :] * u0[0, edge, own : own + 1, :]
            plane[row : row + 1, :] = jnp.where(inside, value, 0.0)

        center, lateral = sides(plane[...], height)
        own = pl.ds(PAD, height)
        centers = [center, u1[1, edge, own, :], u1[2, edge, own, :]]
        beside = lateral + u1[0, within, own, :]
        boundary = relax(factors, edge, 0, centers, beside, forces[0, edge - 1])
        partial = jnp.zeros((1, degrees), jnp.float32)
        for k in range(SLOTS):
            mine = jnp.where(ids[...] == first + k, boundary, 0.0)
            means = jnp.sum(mine, axis=1, keepdims=True) * weights[k]
            partial = partial + jnp.sum(means * basis[k], axis=0, keepdims=True)
        part[lat] = partial

        @pl.loop(1, n_lat)
        def _(i):
            part_copy(i).start()

    def outer_chunk(i):
        row = pl.multiple_of(chunk_of(i) * rows, 8)

        @pl.when(has_above)
        def _():
            rad_down_first(i).wait_recv()

        values = sweep_rows(u0, factors, forces, depth, row, rows)
        for c in range(3):
            u1[c, depth, pl.ds(row + PAD, rows), :] = values[c]

        @pl.when(has_above)
        def _():
            rad_up(i).start()

        @pl.when(has_below)
        def _():
            rad_up_first(i).wait_recv()

        values = sweep_rows(u0, factors, forces, 1, row, rows)
        for c in range(3):
            u1[c, 1, pl.ds(row + PAD, rows), :] = values[c]

        @pl.when(has_below)
        def _():
            rad_down(i).start()

    outer_chunk(0)

    @pl.when(jnp.logical_not(at_end))
    def _():
        take_rows(u0, lat0, all_layers)

    @pl.loop(0, (depth - 2) * CHUNKS)
    def _(i):
        layer = 2 + i // CHUNKS
        row = pl.multiple_of((i % CHUNKS) * rows, 8)
        values = sweep_rows(u0, factors, forces, layer, row, rows)
        for c in range(3):
            u1[c, layer, pl.ds(row + PAD, rows), :] = values[c]

    for side in range(2):
        put_rows(u1, pack1.at[0], side, inner_layers)
    send_up(lat1[0])
    send_down(lat1[0])

    pl.loop(1, CHUNKS - 1)(outer_chunk)
    for side in range(2):
        put_rows(u1, pack1.at[1], side, outer_layers)
    send_up(lat1[1])
    send_down(lat1[1])

    outer_chunk(CHUNKS - 1)

    scale = math.sqrt(2.0 / total)

    @pl.when(at_end)
    def _():
        @pl.loop(1, n_lat)
        def _(i):
            part_arrival(i).wait_recv()

        coef[is_top] = scale * jnp.sum(part[...], axis=0)

        @pl.loop(1, n_rad)
        def _(i):
            coef_copy(i).start()

    take_rows(u1, lat1[0], inner_layers)

    @pl.loop(0, (depth - 2) * CHUNKS)
    def _(i):
        layer = 2 + i // CHUNKS
        row = pl.multiple_of((i % CHUNKS) * rows, 8)
        values = sweep_rows(u1, factors, forces, layer, row, rows)
        for c in range(3):
            smooth_out[c, layer - 1, pl.ds(row, rows), :] = values[c]

    def last_chunk(i):
        row = pl.multiple_of(chunk_of(i) * rows, 8)

        @pl.when(has_above)
        def _():
            rad_down(i).wait_recv()

        values = sweep_rows(u1, factors, forces, depth, row, rows)
        for c in range(3):
            smooth_out[c, depth - 1, pl.ds(row, rows), :] = values[c]

        @pl.when(has_below)
        def _():
            rad_up(i).wait_recv()

        values = sweep_rows(u1, factors, forces, 1, row, rows)
        for c in range(3):
            smooth_out[c, 0, pl.ds(row, rows), :] = values[c]

    last_chunk(0)
    take_rows(u1, lat1[1], outer_layers)
    pl.loop(1, CHUNKS)(last_chunk)

    def coef_arrival(side):
        return remote(
            coef.at[side], coef.at[side], coef_send.at[0], coef_recv.at[side],
            (lat, (rad + 1) % n_rad),
        )

    @pl.when(has_above)
    def _():
        coef_arrival(1).wait_recv()

    @pl.when(has_below)
    def _():
        coef_arrival(0).wait_recv()

    for k in range(2):
        modes = gravity[k, 0:1, :] * coef[1] + gravity[k, 1:2, :] * coef[0]
        values = [
            scale * jnp.sum(basis[s] * modes, axis=1, keepdims=True) for s in range(SLOTS)
        ]
        picked = jnp.where(ids[...] == first + 1, values[1], values[2])
        pot_out[k] = jnp.where(ids[...] == first, values[0], picked)

    leave_lat(lat0)
    for copies in lat1:
        leave_lat(copies)

    @pl.loop(0, CHUNKS)
    def _(i):
        @pl.when(has_above)
        def _():
            rad_up_first(i).wait_send()
            rad_up(i).wait_send()

        @pl.when(has_below)
        def _():
            rad_down_first(i).wait_send()
            rad_down(i).wait_send()

    @pl.when(at_end)
    def _():
        @pl.loop(1, n_lat)
        def _(i):
            part_copy(i).wait_send()

        @pl.loop(1, n_rad)
        def _(i):
            coef_copy(i).wait_send()


def deliver(smooth, pot, smooth_out, pot_out, sems):
    copies = [
        pltpu.make_async_copy(smooth, smooth_out, sems.at[0]),
        pltpu.make_async_copy(pot, pot_out, sems.at[1]),
    ]
    for copy in copies:
        copy.start()
    for copy in copies:
        copy.wait()


def solution(mesh):
    n_lat, n_rad = mesh.shape["lat"], mesh.shape["rad"]

    def local(displacement, forcing, layer_id, stiffness, coupling, cycle_id, cycle_count, gravity):
        _, depth, height, width = displacement.shape
        total = cycle_count.shape[0]
        degrees = gravity.shape[2]
        vmem = pltpu.VMEM
        dma = pltpu.SemaphoreType.DMA
        f32 = jnp.float32
        field = vmem((3, depth + 2, height + 2 * PAD, width), f32)
        anywhere = pl.BlockSpec(memory_space=pl.ANY)
        inside = pl.BlockSpec(memory_space=pltpu.VMEM)
        results = pl.pallas_call(
            functools.partial(kernel, (n_lat, n_rad)),
            out_shape=(
                jax.ShapeDtypeStruct(displacement.shape, f32),
                jax.ShapeDtypeStruct((2, height, width), f32),
            ),
            in_specs=[anywhere] * 8,
            out_specs=(inside, inside),
            scratch_shapes=[
                pltpu.SMEM(layer_id.shape, jnp.int32),
                pltpu.SMEM(stiffness.shape, f32),
                vmem((3, 3, stiffness.shape[0]), f32),
                field,
                field,
                vmem((3, depth, height, width), f32),
                vmem((height, width), jnp.int32),
                vmem((total,), jnp.int32),
                vmem((2, 2, degrees), f32),
                vmem((depth, 16, width), f32),
                vmem((SLOTS, height, degrees), f32),
                vmem((height + 2 * PAD, width), f32),
                vmem((2, 16, width), f32),
                vmem((2, 16, width), f32),
                vmem((2, 2, 8, width), f32),
                vmem((2, 2, 8, width), f32),
                vmem((SLOTS, height, 1), f32),
                vmem((n_lat, 1, degrees), f32),
                vmem((2, 1, degrees), f32),
                dma((8,)),
                dma((2,)), dma((2,)),
                dma((2, CHUNKS)), dma((2, CHUNKS)), dma((2, CHUNKS)), dma((2, CHUNKS)),
                dma((2, 2)), dma((2, 2)),
                dma((n_lat,)), dma((n_lat,)),
                dma((n_rad,)), dma((2,)),
            ],
            compiler_params=pltpu.CompilerParams(
                collective_id=0, has_side_effects=True, vmem_limit_bytes=40 << 20
            ),
        )(*(
            pltpu.with_memory_space_constraint(array, pltpu.HBM)
            for array in (
                displacement, forcing, cycle_id, cycle_count, gravity,
                layer_id, stiffness, jnp.transpose(coupling, (1, 2, 0)),
            )
        ))
        return tuple(pl.pallas_call(
            deliver,
            out_shape=tuple(jax.ShapeDtypeStruct(array.shape, f32) for array in results),
            in_specs=[inside, inside],
            out_specs=(anywhere, anywhere),
            scratch_shapes=[dma((2,))],
            compiler_params=pltpu.CompilerParams(vmem_limit_bytes=1 << 20),
        )(*results))

    in_specs = (
        P(None, "rad", "lat", None),
        P(None, "rad", "lat", None),
        P("rad"),
        P(),
        P(),
        P("lat", None),
        P(),
        P(),
    )
    out_specs = (P(None, "rad", "lat", None), P(None, "lat", None))
    return jax.shard_map(local, mesh=mesh, in_specs=in_specs, out_specs=out_specs, check_vma=False)
```

```python
import functools
import math

import jax
import jax.numpy as jnp
from jax import lax
from jax.experimental import pallas as pl
from jax.experimental.pallas import tpu as pltpu
from jax.sharding import PartitionSpec as P

OMEGA = 0.8
PAD = 8
CHUNKS = 4
SLOTS = 3
MESH = pl.DeviceIdType.MESH


def sides(padded, rows):
    width = padded.shape[1]
    up = pltpu.roll(padded, 1, 0)[PAD : PAD + rows]
    down = pltpu.roll(padded, rows + 2 * PAD - 1, 0)[PAD : PAD + rows]
    center = padded[PAD : PAD + rows]
    column = lax.broadcasted_iota(jnp.int32, center.shape, 1)
    left = jnp.where(column == 0, 0.0, pltpu.roll(center, 1, 1))
    right = jnp.where(column == width - 1, 0.0, pltpu.roll(center, width - 1, 1))
    return center, (up + down) + (left + right)


def relax(factors, layer, c, centers, beside, source):
    def factor(t):
        return factors[layer - 1, 4 * c + t : 4 * c + t + 1, :]

    own = (1.0 - OMEGA) * centers[c] + factor(0) * beside + factor(1) * source
    return own + factor(2) * centers[(c + 1) % 3] + factor(3) * centers[(c + 2) % 3]


def sweep_rows(field, factors, forces, layer, row, rows, components=(0, 1, 2)):
    inner = pl.ds(row + PAD, rows)
    centers, besides = [], []
    for c in range(3):
        if c not in components:
            centers.append(field[c, layer, inner, :])
            besides.append(None)
            continue
        padded = field[c, layer, pl.ds(row, rows + 2 * PAD), :]
        center, lateral = sides(padded, rows)
        besides.append(lateral + (field[c, layer - 1, inner, :] + field[c, layer + 1, inner, :]))
        centers.append(center)
    return [
        relax(factors, layer, c, centers, besides[c], forces[c, layer - 1, pl.ds(row, rows), :])
        for c in components
    ]


def ring(offset, size):
    return min(offset, size - offset)


def rad_hops(offset):
    return ring(offset // 8, 4) + 3 * ring(offset // 2 % 4, 4)


def lat_hops(offset):
    return ring(offset % 8, 8) + ring(offset // 8, 3)


def sine(z):
    z2 = z * z
    poly = 1.0
    for k in (6, 5, 4, 3, 2, 1):
        poly = 1.0 - poly * z2 * (1.0 / ((2 * k) * (2 * k + 1)))
    return z * poly


def kernel(
    sizes,
    disp, force, ids_in, count_in, gravity_in, layer_in, stiffness_in, coupling_in,
    smooth_out, pot_out,
    layer_id, stiffness, coupling, u0, u1, forces, ids, counts, gravity, factors, basis, plane, pack0, halo0,
    pack1, halo1, weights, part, coef,
    load_sem, lat0_send, lat0_recv, rad0_send, rad0_recv,
    rad1_send, rad1_recv, lat1_send, lat1_recv, part_send, part_recv,
    coef_send, coef_recv,
):
    n_lat, n_rad = sizes
    depth, height = disp.shape[1], disp.shape[2]
    total = counts.shape[0]
    degrees = gravity.shape[2]
    rows = height // CHUNKS
    top = height + PAD
    lat = lax.axis_index("lat")
    rad = lax.axis_index("rad")
    has_low, has_high = lat > 0, lat < n_lat - 1
    has_below, has_above = rad > 0, rad < n_rad - 1
    at_end = jnp.logical_or(rad == 0, rad == n_rad - 1)
    is_top = rad // (n_rad - 1)
    edge = 1 + (depth - 1) * is_top
    within = 2 + (depth - 3) * is_top
    barrier = pltpu.get_barrier_semaphore()

    def greet(where):
        pl.semaphore_signal(barrier, inc=1, device_id=where, device_id_type=MESH)

    def remote(src, dst, send, recv, where):
        return pltpu.make_async_remote_copy(
            src_ref=src, dst_ref=dst, send_sem=send, recv_sem=recv,
            device_id=where, device_id_type=MESH,
        )

    loads = [
        pltpu.make_async_copy(disp, u0.at[:, 1 : depth + 1, PAD:top, :], load_sem.at[0]),
        pltpu.make_async_copy(force, forces, load_sem.at[1]),
        pltpu.make_async_copy(ids_in, ids, load_sem.at[2]),
        pltpu.make_async_copy(count_in, counts, load_sem.at[3]),
        pltpu.make_async_copy(gravity_in, gravity, load_sem.at[4]),
        pltpu.make_async_copy(layer_in, layer_id, load_sem.at[5]),
        pltpu.make_async_copy(stiffness_in, stiffness, load_sem.at[6]),
        pltpu.make_async_copy(coupling_in, coupling, load_sem.at[7]),
    ]

    @pl.when(has_low)
    def _():
        greet((lat - 1, rad))

    @pl.when(has_high)
    def _():
        greet((lat + 1, rad))

    @pl.when(has_below)
    def _():
        greet((lat, rad - 1))
        greet((lat, 0))

    @pl.when(has_above)
    def _():
        greet((lat, rad + 1))
        greet((lat, n_rad - 1))

    @pl.when(at_end)
    def _():
        @pl.loop(1, n_lat)
        def _(i):
            greet(((lat + i) % n_lat, rad))

    for load in loads[5:] + loads[:5]:
        load.start()

    for field in (u0, u1):
        @pl.when(jnp.logical_not(has_low))
        def _():
            field[:, 1 : depth + 1, 0:PAD, :] = jnp.zeros((3, depth, PAD, disp.shape[3]), jnp.float32)

        @pl.when(jnp.logical_not(has_high))
        def _():
            field[:, 1 : depth + 1, top : top + PAD, :] = jnp.zeros((3, depth, PAD, disp.shape[3]), jnp.float32)

        @pl.when(jnp.logical_not(has_below))
        def _():
            field[:, 0] = jnp.zeros((3, top + PAD, disp.shape[3]), jnp.float32)

        @pl.when(jnp.logical_not(has_above))
        def _():
            field[:, depth + 1] = jnp.zeros((3, top + PAD, disp.shape[3]), jnp.float32)

    for load in loads[5:]:
        load.wait()

    wide = (1, disp.shape[3])
    materials = lax.broadcasted_iota(jnp.int32, (3, coupling.shape[2]), 1)
    for r in range(depth):
        mu = jnp.full(wide, stiffness[layer_id[r]], jnp.float32)
        for c in range(3):
            row = jnp.sum(
                jnp.where(materials == layer_id[r], coupling[c], 0.0), axis=1, keepdims=True
            )

            def pair(d):
                return jnp.broadcast_to(row[d : d + 1], wide)

            scale = OMEGA / (6.0 * mu + pair(c))
            factors[r, 4 * c : 4 * c + 1, :] = scale * mu
            factors[r, 4 * c + 1 : 4 * c + 2, :] = scale
            factors[r, 4 * c + 2 : 4 * c + 3, :] = -scale * pair((c + 1) % 3)
            factors[r, 4 * c + 3 : 4 * c + 4, :] = -scale * pair((c + 2) % 3)

    below = (rad + n_rad - 1) // n_rad
    above = (2 * n_rad - 2 - rad) // n_rad
    lateral = (lat + n_lat - 1) // n_lat + (2 * n_lat - 2 - lat) // n_lat
    peers = (n_lat - 1) + (n_rad - 1)

    def lat_up(pack, halo, send, recv):
        return remote(pack.at[0], halo.at[0], send.at[0], recv.at[0], (lat + 1, rad))

    def lat_down(pack, halo, send, recv):
        return remote(pack.at[1], halo.at[1], send.at[1], recv.at[1], (lat - 1, rad))

    lat0 = (pack0, halo0, lat0_send, lat0_recv)
    lat1 = [
        (pack1.at[part], halo1.at[part], lat1_send.at[part], lat1_recv.at[part])
        for part in range(2)
    ]
    all_layers = tuple(range(1, depth + 1))
    inner_layers, outer_layers = all_layers[1:-1], (1, depth)

    def planes(layers):
        return [(c, layer) for c in range(3) for layer in layers]

    def put_rows(field, pack, side, layers):
        row = PAD if side else top - 1
        for place, (c, layer) in enumerate(planes(layers)):
            pack[side, place : place + 1, :] = field[c, layer, row : row + 1, :]

    def take_rows(field, copies, layers):
        halo = copies[1]

        @pl.when(has_low)
        def _():
            lat_up(*copies).wait_recv()
            for place, (c, layer) in enumerate(planes(layers)):
                field[c, layer, PAD - 1 : PAD, :] = halo[0, place : place + 1, :]

        @pl.when(has_high)
        def _():
            lat_down(*copies).wait_recv()
            for place, (c, layer) in enumerate(planes(layers)):
                field[c, layer, top : top + 1, :] = halo[1, place : place + 1, :]

    def send_up(copies):
        @pl.when(has_high)
        def _():
            lat_up(*copies).start()

    def send_down(copies):
        @pl.when(has_low)
        def _():
            lat_down(*copies).start()

    def leave_lat(copies):
        @pl.when(has_high)
        def _():
            lat_up(*copies).wait_send()

        @pl.when(has_low)
        def _():
            lat_down(*copies).wait_send()

    def chunk_of(i):
        return i + 1 - 2 * (i % 2)

    def rad_up(i):
        at = pl.ds(pl.multiple_of(PAD + chunk_of(i) * rows, 8), rows)
        return remote(
            u1.at[:, depth, at, :], u1.at[:, 0, at, :],
            rad1_send.at[0, i], rad1_recv.at[0, i], (lat, rad + 1),
        )

    def rad_up_first(i):
        start = chunk_of(i) * rows
        return remote(
            disp.at[:, depth - 1, pl.ds(start, rows), :],
            u0.at[:, 0, pl.ds(pl.multiple_of(PAD + start, 8), rows), :],
            rad0_send.at[0, i], rad0_recv.at[0, i], (lat, rad + 1),
        )

    def rad_down_first(i):
        start = chunk_of(i) * rows
        return remote(
            disp.at[:, 0, pl.ds(start, rows), :],
            u0.at[:, depth + 1, pl.ds(pl.multiple_of(PAD + start, 8), rows), :],
            rad0_send.at[1, i], rad0_recv.at[1, i], (lat, rad - 1),
        )

    def rad_down(i):
        at = pl.ds(pl.multiple_of(PAD + chunk_of(i) * rows, 8), rows)
        return remote(
            u1.at[:, 1, at, :], u1.at[:, depth + 1, at, :],
            rad1_send.at[1, i], rad1_recv.at[1, i], (lat, rad - 1),
        )

    pl.semaphore_wait(barrier, lateral + below + above + (1 - below * above) * peers)
    def send_first(chunks):
        for i in chunks:
            @pl.when(has_above)
            def _():
                rad_up_first(i).start()

            @pl.when(has_below)
            def _():
                rad_down_first(i).start()

    send_first(range(1))
    for load in loads[:5]:
        load.wait()

    spare = 3 * depth
    for side in range(2):
        put_rows(u0, pack0, side, all_layers)

    @pl.when(at_end)
    def _():
        for side, start in ((0, top - PAD), (1, PAD)):
            tile = pl.ds(start, PAD)
            centers = [u0[c, edge, tile, :] for c in range(3)]
            column = lax.broadcasted_iota(jnp.int32, centers[0].shape, 1)
            width = column.shape[1]
            left = jnp.where(column == 0, 0.0, pltpu.roll(centers[0], 1, 1))
            right = jnp.where(column == width - 1, 0.0, pltpu.roll(centers[0], width - 1, 1))
            along = pltpu.roll(centers[0], PAD - 1 if side else 1, 0)
            beside = along + (left + right) + u0[0, within, tile, :]
            value = relax(
                factors, edge, 0, centers, beside, forces[0, edge - 1, pl.ds(start - PAD, PAD), :]
            )
            pick = 0 if side else PAD - 1
            pack0[side, spare : spare + 1, :] = value[pick : pick + 1]

    send_up(lat0)
    send_down(lat0)
    send_first(range(1, CHUNKS))

    first = ids[:, 0:1]
    degree = lax.broadcasted_iota(jnp.int32, (height, degrees), 1).astype(jnp.float32)
    period = 4.0 * total
    for k in range(SLOTS):
        odd = (2 * (first + k) + 1).astype(jnp.float32)
        phase = degree * odd
        phase = phase - period * jnp.floor(phase * (1.0 / period) + 0.5)
        basis[k] = sine((total - jnp.abs(phase)) * (math.pi / (2.0 * total)))

    @pl.when(at_end)
    def _():
        cycle = lax.broadcasted_iota(jnp.int32, (height, total), 1)
        for k in range(SLOTS):
            found = jnp.where(cycle == first + k, counts[...].reshape(1, total), 0)
            count = jnp.sum(found.astype(jnp.float32), axis=1, keepdims=True)
            weights[k] = jnp.where(count > 0.0, 1.0 / jnp.maximum(count, 1.0), 0.0)

    def part_copy(i):
        return remote(
            part.at[lat], part.at[lat], part_send.at[i], part_recv.at[lat],
            ((lat + i) % n_lat, rad),
        )

    def part_arrival(i):
        other = (lat + i) % n_lat
        return remote(
            part.at[other], part.at[other], part_send.at[i], part_recv.at[other], (other, rad)
        )

    def coef_copy(i):
        return remote(
            coef.at[is_top], coef.at[is_top], coef_send.at[i], coef_recv.at[is_top],
            (lat, i + is_top * (n_rad - 1 - 2 * i)),
        )

    @pl.when(at_end)
    def _():
        take_rows(u0, lat0, all_layers)

        @pl.loop(0, CHUNKS)
        def _(i):
            row = pl.multiple_of(i * rows, 8)
            values = sweep_rows(u0, factors, forces, edge, row, rows)
            for c in range(3):
                u1[c, edge, pl.ds(row + PAD, rows), :] = values[c]
            plane[pl.ds(row + PAD, rows), :] = values[0]
            values = sweep_rows(u0, factors, forces, within, row, rows, (0,))
            u1[0, within, pl.ds(row + PAD, rows), :] = values[0]

        for side, inside, row, own in ((0, has_low, PAD - 1, PAD), (1, has_high, top, top - 1)):
            value = halo0[side, spare : spare + 1, :]
            value = value + factors[edge - 1, 0:1, :] * u0[0, edge, own : own + 1, :]
            plane[row : row + 1, :] = jnp.where(inside, value, 0.0)

        center, lateral = sides(plane[...], height)
        own = pl.ds(PAD, height)
        centers = [center, u1[1, edge, own, :], u1[2, edge, own, :]]
        beside = lateral + u1[0, within, own, :]
        boundary = relax(factors, edge, 0, centers, beside, forces[0, edge - 1])
        partial = jnp.zeros((1, degrees), jnp.float32)
        for k in range(SLOTS):
            mine = jnp.where(ids[...] == first + k, boundary, 0.0)
            means = jnp.sum(mine, axis=1, keepdims=True) * weights[k]
            partial = partial + jnp.sum(means * basis[k], axis=0, keepdims=True)
        part[lat] = partial

        for i in sorted(range(1, n_lat), key=lat_hops, reverse=True):
            part_copy(i).start()

    def outer_chunk(i):
        row = pl.multiple_of(chunk_of(i) * rows, 8)

        @pl.when(has_above)
        def _():
            rad_down_first(i).wait_recv()

        values = sweep_rows(u0, factors, forces, depth, row, rows)
        for c in range(3):
            u1[c, depth, pl.ds(row + PAD, rows), :] = values[c]

        @pl.when(has_above)
        def _():
            rad_up(i).start()

        @pl.when(has_below)
        def _():
            rad_up_first(i).wait_recv()

        values = sweep_rows(u0, factors, forces, 1, row, rows)
        for c in range(3):
            u1[c, 1, pl.ds(row + PAD, rows), :] = values[c]

        @pl.when(has_below)
        def _():
            rad_down(i).start()

    outer_chunk(0)

    @pl.when(jnp.logical_not(at_end))
    def _():
        take_rows(u0, lat0, all_layers)

    @pl.loop(0, (depth - 2) * CHUNKS)
    def _(i):
        layer = 2 + i // CHUNKS
        row = pl.multiple_of((i % CHUNKS) * rows, 8)
        values = sweep_rows(u0, factors, forces, layer, row, rows)
        for c in range(3):
            u1[c, layer, pl.ds(row + PAD, rows), :] = values[c]

    for side in range(2):
        put_rows(u1, pack1.at[0], side, inner_layers)
    send_up(lat1[0])
    send_down(lat1[0])

    pl.loop(1, CHUNKS - 1)(outer_chunk)
    for side in range(2):
        put_rows(u1, pack1.at[1], side, outer_layers)
    send_up(lat1[1])
    send_down(lat1[1])

    outer_chunk(CHUNKS - 1)

    scale = math.sqrt(2.0 / total)

    @pl.when(at_end)
    def _():
        @pl.loop(1, n_lat)
        def _(i):
            part_arrival(i).wait_recv()

        coef[is_top] = scale * jnp.sum(part[...], axis=0)

        for i in sorted(range(1, n_rad), key=rad_hops, reverse=True):
            coef_copy(i).start()

    take_rows(u1, lat1[0], inner_layers)

    @pl.loop(0, (depth - 2) * CHUNKS)
    def _(i):
        layer = 2 + i // CHUNKS
        row = pl.multiple_of((i % CHUNKS) * rows, 8)
        values = sweep_rows(u1, factors, forces, layer, row, rows)
        for c in range(3):
            smooth_out[c, layer - 1, pl.ds(row, rows), :] = values[c]

    def last_chunk(i):
        row = pl.multiple_of(chunk_of(i) * rows, 8)

        @pl.when(has_above)
        def _():
            rad_down(i).wait_recv()

        values = sweep_rows(u1, factors, forces, depth, row, rows)
        for c in range(3):
            smooth_out[c, depth - 1, pl.ds(row, rows), :] = values[c]

        @pl.when(has_below)
        def _():
            rad_up(i).wait_recv()

        values = sweep_rows(u1, factors, forces, 1, row, rows)
        for c in range(3):
            smooth_out[c, 0, pl.ds(row, rows), :] = values[c]

    last_chunk(0)
    take_rows(u1, lat1[1], outer_layers)
    pl.loop(1, CHUNKS)(last_chunk)

    def coef_arrival(side):
        return remote(
            coef.at[side], coef.at[side], coef_send.at[0], coef_recv.at[side],
            (lat, (rad + 1) % n_rad),
        )

    @pl.when(has_above)
    def _():
        coef_arrival(1).wait_recv()

    @pl.when(has_below)
    def _():
        coef_arrival(0).wait_recv()

    for k in range(2):
        modes = gravity[k, 0:1, :] * coef[1] + gravity[k, 1:2, :] * coef[0]
        values = [
            scale * jnp.sum(basis[s] * modes, axis=1, keepdims=True) for s in range(SLOTS)
        ]
        picked = jnp.where(ids[...] == first + 1, values[1], values[2])
        pot_out[k] = jnp.where(ids[...] == first, values[0], picked)

    leave_lat(lat0)
    for copies in lat1:
        leave_lat(copies)

    @pl.loop(0, CHUNKS)
    def _(i):
        @pl.when(has_above)
        def _():
            rad_up_first(i).wait_send()
            rad_up(i).wait_send()

        @pl.when(has_below)
        def _():
            rad_down_first(i).wait_send()
            rad_down(i).wait_send()

    @pl.when(at_end)
    def _():
        @pl.loop(1, n_lat)
        def _(i):
            part_copy(i).wait_send()

        @pl.loop(1, n_rad)
        def _(i):
            coef_copy(i).wait_send()


def deliver(smooth, pot, smooth_out, pot_out, sems):
    copies = [
        pltpu.make_async_copy(smooth, smooth_out, sems.at[0]),
        pltpu.make_async_copy(pot, pot_out, sems.at[1]),
    ]
    for copy in copies:
        copy.start()
    for copy in copies:
        copy.wait()


def solution(mesh):
    n_lat, n_rad = mesh.shape["lat"], mesh.shape["rad"]

    def local(displacement, forcing, layer_id, stiffness, coupling, cycle_id, cycle_count, gravity):
        _, depth, height, width = displacement.shape
        total = cycle_count.shape[0]
        degrees = gravity.shape[2]
        vmem = pltpu.VMEM
        dma = pltpu.SemaphoreType.DMA
        f32 = jnp.float32
        field = vmem((3, depth + 2, height + 2 * PAD, width), f32)
        anywhere = pl.BlockSpec(memory_space=pl.ANY)
        inside = pl.BlockSpec(memory_space=pltpu.VMEM)
        results = pl.pallas_call(
            functools.partial(kernel, (n_lat, n_rad)),
            out_shape=(
                jax.ShapeDtypeStruct(displacement.shape, f32),
                jax.ShapeDtypeStruct((2, height, width), f32),
            ),
            in_specs=[anywhere] * 8,
            out_specs=(inside, inside),
            scratch_shapes=[
                pltpu.SMEM(layer_id.shape, jnp.int32),
                pltpu.SMEM(stiffness.shape, f32),
                vmem((3, 3, stiffness.shape[0]), f32),
                field,
                field,
                vmem((3, depth, height, width), f32),
                vmem((height, width), jnp.int32),
                vmem((total,), jnp.int32),
                vmem((2, 2, degrees), f32),
                vmem((depth, 16, width), f32),
                vmem((SLOTS, height, degrees), f32),
                vmem((height + 2 * PAD, width), f32),
                vmem((2, 16, width), f32),
                vmem((2, 16, width), f32),
                vmem((2, 2, 8, width), f32),
                vmem((2, 2, 8, width), f32),
                vmem((SLOTS, height, 1), f32),
                vmem((n_lat, 1, degrees), f32),
                vmem((2, 1, degrees), f32),
                dma((8,)),
                dma((2,)), dma((2,)),
                dma((2, CHUNKS)), dma((2, CHUNKS)), dma((2, CHUNKS)), dma((2, CHUNKS)),
                dma((2, 2)), dma((2, 2)),
                dma((n_lat,)), dma((n_lat,)),
                dma((n_rad,)), dma((2,)),
            ],
            compiler_params=pltpu.CompilerParams(
                collective_id=0, has_side_effects=True, vmem_limit_bytes=40 << 20
            ),
        )(*(
            pltpu.with_memory_space_constraint(array, pltpu.HBM)
            for array in (
                displacement, forcing, cycle_id, cycle_count, gravity,
                layer_id, stiffness, jnp.transpose(coupling, (1, 2, 0)),
            )
        ))
        return tuple(pl.pallas_call(
            deliver,
            out_shape=tuple(jax.ShapeDtypeStruct(array.shape, f32) for array in results),
            in_specs=[inside, inside],
            out_specs=(anywhere, anywhere),
            scratch_shapes=[dma((2,))],
            compiler_params=pltpu.CompilerParams(vmem_limit_bytes=1 << 20),
        )(*results))

    in_specs = (
        P(None, "rad", "lat", None),
        P(None, "rad", "lat", None),
        P("rad"),
        P(),
        P(),
        P("lat", None),
        P(),
        P(),
    )
    out_specs = (P(None, "rad", "lat", None), P(None, "lat", None))
    return jax.shard_map(local, mesh=mesh, in_specs=in_specs, out_specs=out_specs, check_vma=False)
```
